256 devices in a mesh: tile: 32 (over z_lo, y, core), lev: 8 (over x, z_hi).
Axes of the slice: x: 4, y: 4, z: 8 (z_hi: 2, z_lo: 4; z = z_hi * 4 + z_lo), core: 2. Of those that a mesh axis runs over, the one named last changes fastest.
Arguments:
- costate_ending_fields: float32 [4, 16, 32, 32, 128], P(None, 'lev', 'tile'), may hold values from -6 to 6
- costate_ending_elevation: float32 [32, 32, 128], P('tile'), may hold values from -6 to 6
- upstream_transport_coefficient: float32 [16, 32, 32, 128], P('lev', 'tile'), may hold values from 0.05 to 0.45
- eastward_spread_coefficient: float32 [32, 32, 128], P('tile'), may hold values from 0.02 to 0.2
- interface_blending_coefficient: float32 [16, 32, 32, 128], P('lev', 'tile'), may hold values from 0.02 to 0.3
- thickness_sensitivity: float32 [4, 16, 32, 32, 128], P(None, 'lev', 'tile'), may hold values from -1.75 to 1.75
- layer_velocity_factor: float32 [16, 32, 32, 128], P('lev', 'tile'), may hold values from 0.02 to 0.1
- western_join_turned: int32 [32], replicated, may hold values from 0 to 1
- predicted_thermal_skin: float32 [32, 32, 128], P('tile'), may hold values from -6 to 6
- predicted_elevation: float32 [32, 32, 128], P('tile'), may hold values from -6 to 6
- measured_quantity: float32 [8, 32, 32, 512], P('lev', 'tile'), may hold values from -6 to 6
- measurement_precision: float32 [8, 32, 32, 512], P('lev', 'tile'), may hold values from 0.05 to 0.3
- measurement_sort: int32 [8, 32, 32, 512], P('lev', 'tile'), may hold values from 0 to 1
- sampled_location: int32 [8, 32, 32, 512], P('lev', 'tile'), may hold values from 0 to 4095
- active_entry_numbers: int32 [8, 32, 32], P('lev', 'tile'), may hold values from 0 to 512, as said below
Outputs:
- adj_state_start: float32 [4, 16, 32, 32, 128], P(None, 'lev', 'tile')
- adj_height_start: float32 [32, 32, 128], P('tile')
The draws below stay inside these ranges and needn't reach their ends.
Inputs may be any that keep to these rules, and one draw needn't show every extreme that they name: `western_join_turned`: 1 means a rotated seam. `active_entry_numbers`: slots at or above the count carry no record; in every draw some destination tile has all 512 slots live from every source tile in every level group.
All inputs are finite; a program needn't handle non-finite values.
Results may differ from the reference program's by a relative error of at most 0.0003.
Values sent between devices are 32-bit elements; how exact they have to be, the bound alone decides.
No kernel may reach another device: no remote copies, remote signals or barrier semaphores. Data moves between devices by JAX's collectives and lax.ppermute only.
A program may use at most 64 MiB of HBM per device.

```python
import math
from functools import partial
import jax
import jax.numpy as jnp
from jax import lax

NFLD = 4
POINTS_ALONG_X = 32
POINTS_ALONG_Y = 128
CAP = 512
FACET_NUMBER = 32
LGROUPS = 8
LEVELS = 16


def draw_active_entry_numbers(key, part):
    key_base = jax.random.fold_in(key, 11)
    key_busy = jax.random.fold_in(key, 12)
    key_forced = jax.random.fold_in(key, 13)
    base = jax.random.randint(key_base, (LGROUPS, FACET_NUMBER, FACET_NUMBER), 0, CAP // 2 + 1)
    busy = jax.random.randint(key_busy, (FACET_NUMBER,), 0, 4) == 0
    forced = jax.random.randint(key_forced, (), 0, FACET_NUMBER)
    busy = busy | (jnp.arange(FACET_NUMBER) == forced)
    return jnp.where(busy[None, None, :], CAP, base).astype(jnp.int32)


def place_ends(values, own_key, low, high):
    longest = values.shape.index(max(values.shape))
    spots = []
    for shift in (0, 1):
        where = [jax.random.randint(jax.random.fold_in(own_key, axis), (), 0, length) for axis, length in enumerate(values.shape)]
        where[longest] = (where[longest] + shift) % values.shape[longest]
        spots.append(tuple(where))
    return values.at[spots[0]].set(low).at[spots[1]].set(high)


def shard_levels(key, dims, pieces, low, high):
    gain, own = 1.0, jax.random.fold_in(key, 6)
    for axis_at, parts in pieces:
        steps = jnp.exp(jax.random.uniform(jax.random.fold_in(own, axis_at), (parts,), jnp.float32, low / len(pieces), high / len(pieces)))
        gain = gain * jnp.repeat(steps, dims[axis_at] // parts).reshape([-1 if axis == axis_at else 1 for axis in range(len(dims))])
    return gain


def gaussian(rng, extent, width, reach, shards=(), held_as=jnp.bfloat16):
    values = jax.random.normal(rng, extent, jnp.float32) * width
    if len(shards) > 0:
        values = shard_levels(rng, extent, shards, -0.22, 0.18) * values
    return jnp.clip(values, min=-reach, max=reach).astype(held_as)


def setup_inputs(seed: int = 0) -> dict:
    splits = jax.random.split(jax.random.key(seed), 16)
    costate_ending_fields = gaussian(splits[0], (NFLD, LEVELS, FACET_NUMBER, POINTS_ALONG_X, POINTS_ALONG_Y), 1.0, 6.0, ((1, 8), (2, 32)), jnp.float32)
    costate_ending_elevation = gaussian(splits[1], (FACET_NUMBER, POINTS_ALONG_X, POINTS_ALONG_Y), 1.0, 6.0, ((0, 32),), jnp.float32)
    upstream_transport_coefficient = jnp.clip(0.05 + 0.39999999 * jax.random.uniform(splits[2], (LEVELS, FACET_NUMBER, POINTS_ALONG_X, POINTS_ALONG_Y), jnp.float32) ** shard_levels(splits[2], (LEVELS, FACET_NUMBER, POINTS_ALONG_X, POINTS_ALONG_Y), ((0, 8), (1, 32)), -0.2, 0.2), 0.05, 0.45)
    eastward_spread_coefficient = jnp.clip(0.02 + 0.18 * jax.random.uniform(splits[3], (FACET_NUMBER, POINTS_ALONG_X, POINTS_ALONG_Y), jnp.float32) ** shard_levels(splits[3], (FACET_NUMBER, POINTS_ALONG_X, POINTS_ALONG_Y), ((0, 32),), -0.2, 0.2), 0.02, 0.2)
    interface_blending_coefficient = jnp.clip(jnp.exp(math.log(0.3) - 2.7080503 * jax.random.uniform(splits[4], (LEVELS, FACET_NUMBER, POINTS_ALONG_X, POINTS_ALONG_Y), jnp.float32) ** shard_levels(splits[4], (LEVELS, FACET_NUMBER, POINTS_ALONG_X, POINTS_ALONG_Y), ((0, 8), (1, 32)), -0.2, 0.2)), 0.02, 0.3)
    thickness_sensitivity = gaussian(splits[5], (NFLD, LEVELS, FACET_NUMBER, POINTS_ALONG_X, POINTS_ALONG_Y), 0.3, 1.75, ((1, 8), (2, 32)), jnp.float32)
    layer_velocity_factor = jnp.clip(0.02 + 0.08 * jax.random.uniform(splits[6], (LEVELS, FACET_NUMBER, POINTS_ALONG_X, POINTS_ALONG_Y), jnp.float32) ** shard_levels(splits[6], (LEVELS, FACET_NUMBER, POINTS_ALONG_X, POINTS_ALONG_Y), ((0, 8), (1, 32)), -0.2, 0.2), 0.02, 0.1)
    western_join_turned = place_ends(jax.random.randint(splits[7], (FACET_NUMBER,), 0, 2), jax.random.fold_in(splits[7], 1), 0, 1).astype(jnp.int32)
    predicted_thermal_skin = gaussian(splits[8], (FACET_NUMBER, POINTS_ALONG_X, POINTS_ALONG_Y), 1.0, 6.0, ((0, 32),), jnp.float32)
    predicted_elevation = gaussian(splits[9], (FACET_NUMBER, POINTS_ALONG_X, POINTS_ALONG_Y), 1.0, 6.0, ((0, 32),), jnp.float32)
    measured_quantity = gaussian(splits[10], (LGROUPS, FACET_NUMBER, FACET_NUMBER, CAP), 1.0, 6.0, ((0, 8), (1, 32)), jnp.float32)
    measurement_precision = jnp.clip(jnp.exp(math.log(0.3) - 1.7917595 * jax.random.uniform(splits[11], (LGROUPS, FACET_NUMBER, FACET_NUMBER, CAP), jnp.float32) ** shard_levels(splits[11], (LGROUPS, FACET_NUMBER, FACET_NUMBER, CAP), ((0, 8), (1, 32)), -0.2, 0.2)), 0.05, 0.3)
    measurement_sort = place_ends(jax.random.randint(splits[12], (LGROUPS, FACET_NUMBER, FACET_NUMBER, CAP), 0, 2), jax.random.fold_in(splits[12], 1), 0, 1).astype(jnp.int32)
    sampled_location = place_ends(jax.random.randint(splits[13], (LGROUPS, FACET_NUMBER, FACET_NUMBER, CAP), 0, POINTS_ALONG_X * POINTS_ALONG_Y), jax.random.fold_in(splits[13], 1), 0, (POINTS_ALONG_X * POINTS_ALONG_Y) - 1).astype(jnp.int32)
    active_entry_numbers = draw_active_entry_numbers(jax.random.fold_in(splits[15], 71), 0)
    return dict(costate_ending_fields=costate_ending_fields, costate_ending_elevation=costate_ending_elevation, upstream_transport_coefficient=upstream_transport_coefficient, eastward_spread_coefficient=eastward_spread_coefficient, interface_blending_coefficient=interface_blending_coefficient, thickness_sensitivity=thickness_sensitivity, layer_velocity_factor=layer_velocity_factor, western_join_turned=western_join_turned, predicted_thermal_skin=predicted_thermal_skin, predicted_elevation=predicted_elevation, measured_quantity=measured_quantity, measurement_precision=measurement_precision, measurement_sort=measurement_sort, sampled_location=sampled_location, active_entry_numbers=active_entry_numbers)


SEAM_SIGN = (1.0, 1.0, 1.0, -1.0)
SEAM_ORDER = (0, 1, 3, 2)

def tangent_step(state, height, upstream_transport_coefficient, eastward_spread_coefficient, interface_blending_coefficient, thickness_sensitivity, layer_velocity_factor, western_join_turned):
    sign = jnp.array(SEAM_SIGN, jnp.float32)[:, None, None, None].astype(state.dtype)
    order = jnp.array(SEAM_ORDER, jnp.int32)
    last_col = state[..., -1]
    previous = jnp.roll(last_col, 1, axis=2)
    rotated = (western_join_turned == 1)[None, None, :, None]
    swapped = sign * previous[order][..., ::-1]
    seam_col = jnp.where(rotated, swapped, previous)
    westward = jnp.concatenate([seam_col[..., None], state[..., :-1]], axis=-1)
    advect = upstream_transport_coefficient[None] * (westward - state)
    row_mask = (jnp.arange(POINTS_ALONG_X) < POINTS_ALONG_X - 1).astype(state.dtype)[:, None]
    next_row = jnp.concatenate([state[..., 1:, :], jnp.zeros_like(state[..., :1, :])], axis=-2)
    face_y = eastward_spread_coefficient[None, None] * row_mask * (next_row - state)
    mix_row = face_y - jnp.concatenate([jnp.zeros_like(face_y[..., :1, :]), face_y[..., :-1, :]], axis=-2)
    level_mask = (jnp.arange(LEVELS) < LEVELS - 1).astype(state.dtype)[:, None, None, None]
    next_level = jnp.concatenate([state[:, 1:], jnp.zeros_like(state[:, :1])], axis=1)
    face_z = (interface_blending_coefficient * level_mask)[None] * (next_level - state)
    mix_col = face_z - jnp.concatenate([jnp.zeros_like(face_z[:, :1]), face_z[:, :-1]], axis=1)
    new_state = state + advect + mix_row + mix_col + thickness_sensitivity * height[None, None]
    new_height = height + lax.optimization_barrier(jnp.sum(layer_velocity_factor * state[2], axis=0))
    return (new_state, new_height)

def reference(costate_ending_fields, costate_ending_elevation, upstream_transport_coefficient, eastward_spread_coefficient, interface_blending_coefficient, thickness_sensitivity, layer_velocity_factor, western_join_turned, predicted_thermal_skin, predicted_elevation, measured_quantity, measurement_precision, measurement_sort, sampled_location, active_entry_numbers):
    live = jnp.arange(CAP, dtype=jnp.int32)[None, None, None, :] < active_entry_numbers[..., None]
    dest = jnp.arange(FACET_NUMBER, dtype=jnp.int32)[None, None, :, None]
    linear_position = (dest * (POINTS_ALONG_X * POINTS_ALONG_Y) + sampled_location).astype(jnp.int32)
    marine_dynamics = jnp.where(measurement_sort == 0, predicted_thermal_skin.reshape(-1)[linear_position], predicted_elevation.reshape(-1)[linear_position])
    misfit = jnp.where(live, measurement_precision * (marine_dynamics - measured_quantity), jnp.zeros_like(measured_quantity))
    target = (measurement_sort * (FACET_NUMBER * POINTS_ALONG_X * POINTS_ALONG_Y) + linear_position).astype(jnp.int32).reshape(-1)
    maps = jnp.zeros((2 * FACET_NUMBER * POINTS_ALONG_X * POINTS_ALONG_Y,), costate_ending_fields.dtype).at[target].add(misfit.reshape(-1))
    maps = maps.reshape(2, FACET_NUMBER, POINTS_ALONG_X, POINTS_ALONG_Y)
    lam_state = costate_ending_fields.at[0, 0].add(maps[0])
    lam_height = costate_ending_elevation + maps[1]
    stepper = partial(tangent_step, upstream_transport_coefficient=upstream_transport_coefficient, eastward_spread_coefficient=eastward_spread_coefficient, interface_blending_coefficient=interface_blending_coefficient, thickness_sensitivity=thickness_sensitivity, layer_velocity_factor=layer_velocity_factor, western_join_turned=western_join_turned)
    zero_state = jnp.zeros_like(costate_ending_fields)
    zero_height = jnp.zeros_like(costate_ending_elevation)
    for turn in range(2):
        _, backward = jax.vjp(stepper, zero_state, zero_height)
        lam_state, lam_height = backward((lam_state, lam_height))
    return (lam_state, lam_height)
```

```python
import jax
import jax.numpy as jnp
from jax import lax
from jax.experimental import pallas as pl
from jax.experimental.pallas import tpu as pltpu
from jax.sharding import PartitionSpec as P

OUT_SIGN = (1.0, 1.0, -1.0, 1.0)
SEAM_ORDER = (0, 1, 3, 2)


def shifted(value, axis, steps):
    count = lax.axis_size(axis)
    pairs = [(source, (source + steps) % count) for source in range(count)]
    return lax.ppermute(value, axis, pairs)


def from_behind(block, axis, distance):
    devices = range(lax.axis_size(axis))
    route = [(i - distance, i) for i in devices if i - distance in devices]
    return lax.ppermute(block, axis, route)


PIECES = 3
ROWS_AT_ONCE = 8


def maps_kernel(records, thermal, elevation, out, total):
    sources, slots = records.shape[1:]
    rows, cols = thermal.shape
    half = jnp.bfloat16
    row_of = lax.broadcasted_iota(jnp.int32, (2 * rows, slots), 0).astype(jnp.float32).astype(half)
    col_of = lax.broadcasted_iota(jnp.int32, (cols, slots), 0).astype(jnp.float32).astype(half)
    nothing = jnp.zeros((2 * rows, slots), half)
    one, zero = jnp.ones((cols, slots), half), jnp.zeros((cols, slots), half)
    total[...] = jnp.zeros_like(total)

    def body(i, carry):
        left, right = [], []
        for j in range(ROWS_AT_ONCE):
            weight, scaled, kind, place = (records[n, pl.ds(i * ROWS_AT_ONCE + j, 1), :] for n in range(4))
            row = jnp.floor(place * (1.0 / cols))
            col = place - row * cols
            row = row + kind * rows
            here = jnp.broadcast_to(row.astype(half), nothing.shape) == row_of
            parts = []
            for rest in (weight, scaled):
                for _ in range(PIECES):
                    piece = rest.astype(half)
                    rest = rest - piece.astype(jnp.float32)
                    parts.append(jnp.where(here, jnp.broadcast_to(piece, nothing.shape), nothing))
            left.append(jnp.concatenate(parts, 0))
            right.append(jnp.where(jnp.broadcast_to(col.astype(half), one.shape) == col_of, one, zero))
        total[...] += lax.dot_general(
            jnp.concatenate(left, 1),
            jnp.concatenate(right, 1),
            (((1,), (1,)), ((), ())),
            preferred_element_type=jnp.float32,
        )
        return carry

    lax.fori_loop(0, sources // ROWS_AT_ONCE, body, 0)
    step = 2 * rows
    weights = sum(total[n * step : (n + 1) * step] for n in range(PIECES))
    values = sum(total[n * step : (n + 1) * step] for n in range(PIECES, 2 * PIECES))
    out[0] = thermal[...] * weights[:rows] - values[:rows]
    out[1] = elevation[...] * weights[rows:] - values[rows:]


def local_maps(records, thermal, elevation):
    rows, cols = thermal.shape
    return pl.pallas_call(
        maps_kernel,
        out_shape=jax.ShapeDtypeStruct((2, rows, cols), jnp.float32),
        in_specs=[pl.BlockSpec(memory_space=pltpu.VMEM)] * 3,
        out_specs=pl.BlockSpec(memory_space=pltpu.VMEM),
        scratch_shapes=[pltpu.VMEM((4 * PIECES * rows, cols), jnp.float32)],
        name="maps",
    )(records, thermal, elevation)


def adjoint_step(lam_state, lam_height, flow_l, diff_l, mix_l, stretch_l, weight_l, rotated):
    scaled = flow_l[None] * lam_state
    advect = jnp.concatenate([scaled[..., 1:], jnp.zeros_like(scaled[..., :1])], axis=-1) - scaled
    edge = scaled[..., 0]
    sign = jnp.array(OUT_SIGN, jnp.float32)[:, None, None]
    order = jnp.array(SEAM_ORDER, jnp.int32)
    outgoing = jnp.where(rotated, sign * edge[order][..., ::-1], edge)
    incoming = shifted(outgoing, "tile", -1)
    advect = advect.at[..., -1].add(incoming)
    next_row = jnp.concatenate(
        [lam_state[..., 1:, :], jnp.zeros_like(lam_state[..., :1, :])], axis=-2
    )
    face_y = diff_l[None, None] * (next_row - lam_state)
    mix_row = face_y - jnp.concatenate(
        [jnp.zeros_like(face_y[..., :1, :]), face_y[..., :-1, :]], axis=-2
    )
    below = from_behind(lam_state[:, :1], "lev", -1)
    lower = jnp.concatenate([lam_state[:, 1:], below], axis=1)
    face_z = mix_l[None] * (lower - lam_state)
    above = from_behind(face_z[:, -1:], "lev", 1)
    mix_col = face_z - jnp.concatenate([above, face_z[:, :-1]], axis=1)
    new_state = lam_state + advect + mix_row + mix_col
    new_state = new_state.at[2].add(weight_l * lam_height[None])
    column_part = jnp.sum(stretch_l * lam_state, axis=(0, 1))
    new_height = lam_height + lax.psum(column_part, "lev")
    return (new_state, new_height)


def per_device(
    costate_ending_fields,
    costate_ending_elevation,
    upstream_transport_coefficient,
    eastward_spread_coefficient,
    interface_blending_coefficient,
    thickness_sensitivity,
    layer_velocity_factor,
    western_join_turned,
    predicted_thermal_skin,
    predicted_elevation,
    measured_quantity,
    measurement_precision,
    measurement_sort,
    sampled_location,
    active_entry_numbers,
):
    lev_dev = costate_ending_fields.shape[1]
    rows = costate_ending_fields.shape[3]
    cols = costate_ending_fields.shape[4]
    slots = measured_quantity.shape[3]
    lev_index = lax.axis_index("lev")
    tile_index = lax.axis_index("tile")
    level_total = lev_dev * lax.axis_size("lev")
    global_level = lev_index * lev_dev + jnp.arange(lev_dev, dtype=jnp.int32)
    mix_l = (
        interface_blending_coefficient[:, 0]
        * (global_level < level_total - 1).astype(jnp.float32)[:, None, None]
    )
    row_mask = (jnp.arange(rows) < rows - 1).astype(jnp.float32)[:, None]
    diff_l = eastward_spread_coefficient[0] * row_mask
    flow_l = upstream_transport_coefficient[:, 0]
    stretch_l = thickness_sensitivity[:, :, 0]
    weight_l = layer_velocity_factor[:, 0]
    rotated = western_join_turned[tile_index] == 1
    live = jnp.arange(slots, dtype=jnp.int32)[None, :] < active_entry_numbers[0, 0][:, None]
    weight = jnp.where(live, measurement_precision[0, 0], 0.0)
    packet = jnp.stack(
        [
            weight,
            weight * measured_quantity[0, 0],
            measurement_sort[0, 0].astype(jnp.float32),
            sampled_location[0, 0].astype(jnp.float32),
        ]
    )
    arrived = lax.all_to_all(packet, "tile", split_axis=1, concat_axis=1, tiled=True)
    maps = local_maps(arrived, predicted_thermal_skin[0], predicted_elevation[0])
    maps = lax.psum(maps, "lev")
    lam_state = costate_ending_fields[:, :, 0]
    lam_state = lam_state.at[0, 0].add(jnp.where(lev_index == 0, maps[0], 0.0))
    lam_height = costate_ending_elevation[0] + maps[1]
    for turn in range(2):
        lam_state, lam_height = adjoint_step(
            lam_state, lam_height, flow_l, diff_l, mix_l, stretch_l, weight_l, rotated
        )
    return (lam_state[:, :, None], lam_height[None])


def solution(mesh):
    placed = (
        P(None, "lev", "tile", None, None),
        P("tile", None, None),
        P("lev", "tile", None, None),
        P("tile", None, None),
        P("lev", "tile", None, None),
        P(None, "lev", "tile", None, None),
        P("lev", "tile", None, None),
        P(),
        P("tile", None, None),
        P("tile", None, None),
        P("lev", "tile", None, None),
        P("lev", "tile", None, None),
        P("lev", "tile", None, None),
        P("lev", "tile", None, None),
        P("lev", "tile", None),
    )
    return jax.shard_map(
        per_device,
        mesh=mesh,
        in_specs=placed,
        out_specs=(P(None, "lev", "tile", None, None), P("tile", None, None)),
        check_vma=False,
    )
```

```python
import jax
import jax.numpy as jnp
from jax import lax
from jax.experimental import pallas as pl
from jax.experimental.pallas import tpu as pltpu
from jax.sharding import PartitionSpec as P

FIELDS = 4
LEVELS_HERE = 2
PIECES = 3
ROWS_AT_ONCE = 8
MAP_HEIGHT, MAP_THERMAL, STEP_TWO, STEP_ONE, WEIGHTED, FLOW_TOP, STRETCH_TOP, STRETCH_NEXT, MIX_TOP = range(9)
SUMS = 9


def vmem(count):
    return [pl.BlockSpec(memory_space=pltpu.VMEM)] * count


def maps_kernel(records, thermal, elevation, out, total):
    sources, slots = records.shape[1:]
    rows, cols = thermal.shape
    half = jnp.bfloat16
    row_of = lax.broadcasted_iota(jnp.int32, (2 * rows, slots), 0).astype(jnp.float32).astype(half)
    col_of = lax.broadcasted_iota(jnp.int32, (cols, slots), 0).astype(jnp.float32).astype(half)
    nothing = jnp.zeros((2 * rows, slots), half)
    one, zero = jnp.ones((cols, slots), half), jnp.zeros((cols, slots), half)
    total[...] = jnp.zeros_like(total)

    def body(i, carry):
        left, right = [], []
        for j in range(ROWS_AT_ONCE):
            weight, scaled, kind, place = (records[n, pl.ds(i * ROWS_AT_ONCE + j, 1), :] for n in range(4))
            row = jnp.floor(place * (1.0 / cols))
            col = place - row * cols
            row = row + kind * rows
            here = jnp.broadcast_to(row.astype(half), nothing.shape) == row_of
            parts = []
            for rest in (weight, scaled):
                for _ in range(PIECES):
                    piece = rest.astype(half)
                    rest = rest - piece.astype(jnp.float32)
                    parts.append(jnp.where(here, jnp.broadcast_to(piece, nothing.shape), nothing))
            left.append(jnp.concatenate(parts, 0))
            right.append(jnp.where(jnp.broadcast_to(col.astype(half), one.shape) == col_of, one, zero))
        total[...] += lax.dot_general(
            jnp.concatenate(left, 1),
            jnp.concatenate(right, 1),
            (((1,), (1,)), ((), ())),
            preferred_element_type=jnp.float32,
        )
        return carry

    lax.fori_loop(0, sources // ROWS_AT_ONCE, body, 0)
    step = 2 * rows
    weights = sum(total[n * step : (n + 1) * step] for n in range(PIECES))
    values = sum(total[n * step : (n + 1) * step] for n in range(PIECES, 2 * PIECES))
    out[MAP_THERMAL] = thermal[...] * weights[:rows] - values[:rows]
    out[MAP_HEIGHT] = elevation[...] * weights[rows:] - values[rows:]


def local_maps(records, thermal, elevation):
    rows, cols = thermal.shape
    return pl.pallas_call(
        maps_kernel,
        out_shape=jax.ShapeDtypeStruct((2, rows, cols), jnp.float32),
        in_specs=vmem(3),
        out_specs=vmem(1)[0],
        scratch_shapes=[pltpu.VMEM((4 * PIECES * rows, cols), jnp.float32)],
        name="maps",
    )(records, thermal, elevation)


def along_columns(value, last):
    cols = value.shape[1]
    lane = lax.broadcasted_iota(jnp.int32, value.shape, 1)
    return jnp.where(lane == cols - 1, jnp.broadcast_to(last, value.shape), pltpu.roll(value, cols - 1, 1))


def across_rows(value, spread):
    rows = value.shape[0]
    face = spread * (pltpu.roll(value, rows - 1, 0) - value)
    return face - pltpu.roll(face, 1, 0)


def masked_spread(spread):
    row = lax.broadcasted_iota(jnp.int32, spread.shape, 0)
    return jnp.where(row < spread.shape[0] - 1, spread[...], 0.0)


def horizontal(value, flow, spread, last):
    scaled = flow * value
    return value + (along_columns(scaled, last) - scaled) + across_rows(value, spread)


def to_column(line, rows):
    wide = jnp.broadcast_to(line, (rows, line.shape[1]))
    same = lax.broadcasted_iota(jnp.int32, wide.shape, 0) == lax.broadcasted_iota(jnp.int32, wide.shape, 1)
    return jnp.sum(jnp.where(same, wide, 0.0), axis=1, keepdims=True)


def to_line(value, turned):
    rows = value.shape[0]
    row = lax.broadcasted_iota(jnp.int32, value.shape, 0)
    lane = lax.broadcasted_iota(jnp.int32, value.shape, 1)
    chosen = lane == jnp.where(turned, rows - 1 - row, row)
    return jnp.sum(jnp.where(chosen, jnp.broadcast_to(value[:, :1], value.shape), 0.0), axis=0, keepdims=True)


def edges(state, flow, turned, out):
    for k in range(LEVELS_HERE):
        lines = [to_line(flow[k] * state[f][k], turned) for f in range(FIELDS)]
        lines[2], lines[3] = jnp.where(turned, -lines[3], lines[2]), jnp.where(turned, lines[2], lines[3])
        for f in range(FIELDS):
            out[pl.ds(f * LEVELS_HERE + k, 1), :] = lines[f]


def start_kernel(flags, state, flow, mix, stretch, weight, halo, sums, edge):
    first = flags[0] == 0
    turned = flags[1] == 1
    maps = [[state[f, k] for k in range(LEVELS_HERE)] for f in range(FIELDS)]
    for f in range(FIELDS):
        for k in range(LEVELS_HERE):
            halo[k * FIELDS + f] = maps[f][k]
    halo[8] = weight[0]
    halo[9] = weight[1]
    halo[10] = mix[1]
    column = None
    for f in range(FIELDS):
        for k in range(LEVELS_HERE):
            term = stretch[f, k] * maps[f][k]
            column = term if column is None else column + term
    sums[0] = column
    sums[1] = stretch[2, 0] * weight[0] + stretch[2, 1] * weight[1]
    none = jnp.zeros_like(column)
    sums[2] = jnp.where(first, flow[0], none)
    sums[3] = jnp.where(first, stretch[0, 0], none)
    sums[4] = jnp.where(first, stretch[0, 1], none)
    sums[5] = jnp.where(first, mix[0], none)
    edges(maps, [flow[0], flow[1]], turned, edge)


def lower_mix(mix, flags):
    return jnp.where(flags[0] == flags[2], 0.0, mix[1])


def step_one_kernel(flags, state, flow, mix, stretch, spread, partner, relayed, edge, maps, sums, out):
    rows = spread.shape[0]
    low = flags[3] == 0
    spread_y = masked_spread(spread)
    mix_low = lower_mix(mix, flags)
    mix_high = jnp.where(low, relayed[5], partner[10])
    column = None
    for f in range(FIELDS):
        top, bottom = state[f, 0], state[f, 1]
        below = jnp.where(low, partner[f], relayed[f])
        above = jnp.where(low, relayed[f], partner[FIELDS + f])
        face = mix[0] * (bottom - top)
        new_top = horizontal(top, flow[0], spread_y, to_column(edge[2 * f : 2 * f + 1], rows))
        new_top = new_top + (face - mix_high * (top - above))
        new_bottom = horizontal(bottom, flow[1], spread_y, to_column(edge[2 * f + 1 : 2 * f + 2], rows))
        new_bottom = new_bottom + (mix_low * (below - bottom) - face)
        out[SUMS + f] = new_top
        out[SUMS + FIELDS + f] = new_bottom
        term = stretch[f, 0] * new_top + stretch[f, 1] * new_bottom
        column = term if column is None else column + term
    out[MAP_HEIGHT] = maps[MAP_HEIGHT]
    out[MAP_THERMAL] = maps[MAP_THERMAL]
    out[STEP_TWO] = column
    for n in range(SUMS - 3):
        out[STEP_ONE + n] = sums[n]


def middle_state(flags, own, sums, height, weight, mix, spread_y, last):
    first = flags[0] == 0
    thermal = sums[MAP_THERMAL]
    fields = [[own[k * FIELDS + f] for k in range(LEVELS_HERE)] for f in range(FIELDS)]
    moved = horizontal(thermal, sums[FLOW_TOP], spread_y, last) - sums[MIX_TOP] * thermal
    fields[0][0] = fields[0][0] + jnp.where(first, moved, 0.0)
    fields[0][1] = fields[0][1] + jnp.where(first, mix[0] * thermal, 0.0)
    for k in range(LEVELS_HERE):
        fields[2][k] = fields[2][k] + weight[k] * height
    return fields, moved


def edge_kernel(flags, own, sums, elevation, flow, mix, spread, weight, edge):
    turned = flags[1] == 1
    spread_y = masked_spread(spread)
    height = elevation[...] + sums[MAP_HEIGHT]
    fields, _ = middle_state(
        flags, own, sums, height, weight, mix, spread_y, jnp.zeros((spread.shape[0], 1), jnp.float32)
    )
    edges(fields, [flow[0], flow[1]], turned, edge)
    edge[8:16, :] = jnp.zeros((8, edge.shape[1]), jnp.float32)
    edge[8:9, :] = to_line(sums[FLOW_TOP] * sums[MAP_THERMAL], turned)


def step_two_kernel(
    flags, own, partner, relayed, sums, elevation, flow, mix, spread, weight,
    old_partner, old_relayed, edge, out_state, out_height,
):
    rows = spread.shape[0]
    low = flags[3] == 0
    spread_y = masked_spread(spread)
    mix_low = lower_mix(mix, flags)
    mix_high = jnp.where(low, old_relayed[5], old_partner[10])
    weight_above = jnp.where(low, old_relayed[4], old_partner[9])
    weight_below = jnp.where(low, old_partner[8], old_relayed[4])
    thermal = sums[MAP_THERMAL]
    height = elevation[...] + sums[MAP_HEIGHT]
    fields, moved = middle_state(
        flags, own, sums, height, weight, mix, spread_y, to_column(edge[8:9], rows)
    )
    height_one = height + sums[STEP_ONE] + sums[STRETCH_TOP] * thermal
    for f in range(FIELDS):
        top, bottom = fields[f]
        below = jnp.where(low, partner[f], relayed[f])
        above = jnp.where(low, relayed[f], partner[FIELDS + f])
        if f == 0:
            above = above + jnp.where(flags[0] == 1, sums[MIX_TOP] * thermal, 0.0)
        if f == 2:
            above = above + weight_above * height
            below = below + weight_below * height
        face = mix[0] * (bottom - top)
        new_top = horizontal(top, flow[0], spread_y, to_column(edge[2 * f : 2 * f + 1], rows))
        new_top = new_top + (face - mix_high * (top - above))
        new_bottom = horizontal(bottom, flow[1], spread_y, to_column(edge[2 * f + 1 : 2 * f + 2], rows))
        new_bottom = new_bottom + (mix_low * (below - bottom) - face)
        if f == 2:
            new_top = new_top + weight[0] * height_one
            new_bottom = new_bottom + weight[1] * height_one
        out_state[f, 0] = new_top
        out_state[f, 1] = new_bottom
    out_height[...] = (
        height_one
        + sums[STEP_TWO]
        + sums[WEIGHTED] * height
        + sums[STRETCH_TOP] * moved
        + sums[STRETCH_NEXT] * (sums[MIX_TOP] * thermal)
    )


def call(kernel, flags, operands, shapes, name):
    return pl.pallas_call(
        kernel,
        out_shape=[jax.ShapeDtypeStruct(shape, jnp.float32) for shape in shapes],
        in_specs=[pl.BlockSpec(memory_space=pltpu.SMEM)] + vmem(len(operands)),
        out_specs=vmem(len(shapes)),
        name=name,
    )(flags, *operands)


def per_device(
    costate_ending_fields,
    costate_ending_elevation,
    upstream_transport_coefficient,
    eastward_spread_coefficient,
    interface_blending_coefficient,
    thickness_sensitivity,
    layer_velocity_factor,
    western_join_turned,
    predicted_thermal_skin,
    predicted_elevation,
    measured_quantity,
    measurement_precision,
    measurement_sort,
    sampled_location,
    active_entry_numbers,
):
    rows = costate_ending_fields.shape[3]
    cols = costate_ending_fields.shape[4]
    slots = measured_quantity.shape[3]
    groups = lax.axis_size("lev")
    tiles = lax.axis_size("tile")
    lev_index = lax.axis_index("lev")
    tile_index = lax.axis_index("tile")
    low = lev_index % 2 == 0
    flip = [(l, l ^ 1) for l in range(groups)]
    pair = [(l, l ^ 2) for l in range(groups)]
    mirror = [(l, groups - 2 - (l & ~1) + (l & 1)) for l in range(groups)]
    relay = [(l, l + 2) for l in range(0, groups - 2, 2)] + [(l, l - 2) for l in range(3, groups, 2)]
    west = [(t, (t - 1) % tiles) for t in range(tiles)]
    flags = jnp.stack([lev_index, western_join_turned[tile_index], jnp.int32(groups - 1), lev_index % 2])

    state = costate_ending_fields[:, :, 0]
    elevation = costate_ending_elevation[0]
    flow = upstream_transport_coefficient[:, 0]
    spread = eastward_spread_coefficient[0]
    mix = interface_blending_coefficient[:, 0]
    stretch = thickness_sensitivity[:, :, 0]
    weight = layer_velocity_factor[:, 0]

    live = jnp.arange(slots, dtype=jnp.int32)[None, :] < active_entry_numbers[0, 0][:, None]
    precision = jnp.where(live, measurement_precision[0, 0], 0.0)
    packet = jnp.stack(
        [
            precision,
            precision * measured_quantity[0, 0],
            measurement_sort[0, 0].astype(jnp.float32),
            sampled_location[0, 0].astype(jnp.float32),
        ]
    )
    arrived = lax.all_to_all(packet, "tile", split_axis=1, concat_axis=1, tiled=True)

    halo, early, edge = call(
        start_kernel, flags, (state, flow, mix, stretch, weight),
        [(11, rows, cols), (SUMS - 3, rows, cols), (8, cols)], "start",
    )
    edge = lax.ppermute(edge, "tile", west)
    old_partner = lax.ppermute(halo, "lev", flip)
    passed = jnp.concatenate(
        [
            jnp.where(low, old_partner[FIELDS : 2 * FIELDS], old_partner[:FIELDS]),
            jnp.where(low, old_partner[9:10], old_partner[8:9]),
            old_partner[10:11],
        ]
    )
    old_relayed = lax.ppermute(passed, "lev", relay)

    maps = local_maps(arrived, predicted_thermal_skin[0], predicted_elevation[0])
    (mine,) = call(
        step_one_kernel, flags,
        (state, flow, mix, stretch, spread, old_partner, old_relayed, edge, maps, early),
        [(SUMS + 2 * FIELDS, rows, cols)], "step_one",
    )
    theirs = lax.ppermute(mine, "lev", flip)
    partner = theirs[SUMS:]
    relayed = lax.ppermute(jnp.where(low, partner[FIELDS:], partner[:FIELDS]), "lev", relay)
    sums = mine[:SUMS] + theirs[:SUMS]
    sums = sums + lax.ppermute(sums, "lev", pair)
    sums = sums + lax.ppermute(sums, "lev", mirror)
    own = mine[SUMS:]
    (edge,) = call(
        edge_kernel, flags, (own, sums, elevation, flow, mix, spread, weight), [(16, cols)], "edge"
    )
    edge = lax.ppermute(edge, "tile", west)
    out_state, out_height = call(
        step_two_kernel, flags,
        (own, partner, relayed, sums, elevation, flow, mix, spread, weight, old_partner, old_relayed, edge),
        [state.shape, (rows, cols)], "step_two",
    )
    return (out_state[:, :, None], out_height[None])


def solution(mesh):
    placed = (
        P(None, "lev", "tile", None, None),
        P("tile", None, None),
        P("lev", "tile", None, None),
        P("tile", None, None),
        P("lev", "tile", None, None),
        P(None, "lev", "tile", None, None),
        P("lev", "tile", None, None),
        P(),
        P("tile", None, None),
        P("tile", None, None),
        P("lev", "tile", None, None),
        P("lev", "tile", None, None),
        P("lev", "tile", None, None),
        P("lev", "tile", None, None),
        P("lev", "tile", None),
    )
    return jax.shard_map(
        per_device,
        mesh=mesh,
        in_specs=placed,
        out_specs=(P(None, "lev", "tile", None, None), P("tile", None, None)),
        check_vma=False,
    )
```

```python
import jax
import jax.numpy as jnp
from jax import lax
from jax.experimental import pallas as pl
from jax.experimental.pallas import tpu as pltpu
from jax.sharding import PartitionSpec as P

FIELDS = 4
LEVELS_HERE = 2
PIECES = 3
ROWS_AT_ONCE = 8
MAP_HEIGHT, MAP_THERMAL, STEP_TWO = range(3)
STEP_ONE, WEIGHTED, FLOW_TOP, STRETCH_TOP, THERMAL_GAIN = range(5)
EARLY = 5
HALO, MIDDLE = FIELDS + 1, FIELDS + 2


def maps_kernel(records, thermal, elevation, out, total):
    rows, cols = thermal.shape
    sources, _, slots = records.shape
    half = jnp.bfloat16
    row_of = lax.broadcasted_iota(jnp.int32, (2 * rows, slots), 0).astype(jnp.float32).astype(half)
    col_of = lax.broadcasted_iota(jnp.int32, (cols, slots), 0).astype(jnp.float32).astype(half)
    nothing = jnp.zeros((2 * rows, slots), half)
    one, zero = jnp.ones((cols, slots), half), jnp.zeros((cols, slots), half)
    total[...] = jnp.zeros_like(total)

    def body(i, carry):
        left, right = [], []
        for j in range(ROWS_AT_ONCE):
            weight, scaled, kind, place = (
                records[i * ROWS_AT_ONCE + j, n : n + 1, :] for n in range(4)
            )
            row = jnp.floor(place * (1.0 / cols))
            col = place - row * cols
            row = row + kind * rows
            here = jnp.broadcast_to(row.astype(half), nothing.shape) == row_of
            parts = []
            for rest in (weight, scaled):
                for _ in range(PIECES):
                    piece = rest.astype(half)
                    rest = rest - piece.astype(jnp.float32)
                    parts.append(jnp.where(here, jnp.broadcast_to(piece, nothing.shape), nothing))
            left.append(jnp.concatenate(parts, 0))
            right.append(jnp.where(jnp.broadcast_to(col.astype(half), one.shape) == col_of, one, zero))
        total[...] += lax.dot_general(
            jnp.concatenate(left, 1),
            jnp.concatenate(right, 1),
            (((1,), (1,)), ((), ())),
            preferred_element_type=jnp.float32,
        )
        return carry

    lax.fori_loop(0, sources // ROWS_AT_ONCE, body, 0)
    step = 2 * rows
    weights = sum(total[n * step : (n + 1) * step] for n in range(PIECES))
    values = sum(total[n * step : (n + 1) * step] for n in range(PIECES, 2 * PIECES))
    out[MAP_THERMAL] = thermal[...] * weights[:rows] - values[:rows]
    out[MAP_HEIGHT] = elevation[...] * weights[rows:] - values[rows:]


def place(turned_ref):
    lev = lax.axis_index("lev")
    turned = turned_ref[lax.axis_index("tile")] == 1
    return lev, lev == lax.axis_size("lev") - 1, lev % 2 == 0, turned


def along_columns(value, last):
    cols = value.shape[1]
    lane = lax.broadcasted_iota(jnp.int32, value.shape, 1)
    return jnp.where(lane == cols - 1, jnp.broadcast_to(last, value.shape), pltpu.roll(value, cols - 1, 1))


def across_rows(value, spread):
    rows = value.shape[0]
    face = spread * (pltpu.roll(value, rows - 1, 0) - value)
    return face - pltpu.roll(face, 1, 0)


def masked_spread(spread):
    row = lax.broadcasted_iota(jnp.int32, spread.shape, 0)
    return jnp.where(row < spread.shape[0] - 1, spread[...], 0.0)


def horizontal(value, flow, spread, last):
    scaled = flow * value
    return value + (along_columns(scaled, last) - scaled) + across_rows(value, spread)


def to_column(line, rows, shift):
    wide = jnp.broadcast_to(line, (rows, line.shape[1]))
    row = lax.broadcasted_iota(jnp.int32, wide.shape, 0)
    lane = lax.broadcasted_iota(jnp.int32, wide.shape, 1)
    return jnp.sum(jnp.where(lane == row + shift, wide, 0.0), axis=1, keepdims=True)


def to_line(value, turned, shift):
    rows = value.shape[0]
    row = lax.broadcasted_iota(jnp.int32, value.shape, 0)
    lane = lax.broadcasted_iota(jnp.int32, value.shape, 1)
    chosen = lane == shift + jnp.where(turned, rows - 1 - row, row)
    return jnp.sum(jnp.where(chosen, jnp.broadcast_to(value[:, :1], value.shape), 0.0), axis=0, keepdims=True)


def edges(state, flow, turned):
    rows = state[0][0].shape[0]
    lines = [
        sum(to_line(flow[k] * state[f][k], turned, k * rows) for k in range(LEVELS_HERE)) for f in range(FIELDS)
    ]
    lines[2], lines[3] = jnp.where(turned, -lines[3], lines[2]), jnp.where(turned, lines[2], lines[3])
    return lines


def store_lines(lines, out):
    rest = jnp.zeros((out.shape[0] - len(lines), out.shape[1]), jnp.float32)
    out[...] = jnp.concatenate([*lines, rest], 0)


def packet_kernel(counts, measured, precision, kind, location, packet):
    sources, slots = measured.shape
    lane = lax.broadcasted_iota(jnp.int32, (1, slots), 1)
    for s in range(sources):
        weight = jnp.where(lane < counts[s], precision[s : s + 1, :], 0.0)
        packet[s, 0:1, :] = weight
        packet[s, 1:2, :] = weight * measured[s : s + 1, :]
        packet[s, 2:3, :] = kind[s : s + 1, :].astype(jnp.float32)
        packet[s, 3:4, :] = location[s : s + 1, :].astype(jnp.float32)


def start_kernel(turned_ref, state, flow, mix, stretch, weight, to_flip, to_other, early, edge):
    lev, _, low, turned = place(turned_ref)
    first = lev == 0
    column = None
    for f in range(FIELDS):
        top, bottom = state[f, 0], state[f, 1]
        to_flip[f] = jnp.where(low, bottom, top)
        to_other[f] = jnp.where(low, top, bottom)
        term = stretch[f, 0] * top + stretch[f, 1] * bottom
        column = term if column is None else column + term
    to_flip[FIELDS] = mix[1]
    to_other[FIELDS] = mix[1]
    none = jnp.zeros_like(column)
    gain = stretch[0, 0] * (1.0 - flow[0] - mix[0]) + stretch[0, 1] * mix[0]
    early[STEP_ONE] = column
    early[WEIGHTED] = stretch[2, 0] * weight[0] + stretch[2, 1] * weight[1]
    early[FLOW_TOP] = jnp.where(first, flow[0], none)
    early[STRETCH_TOP] = jnp.where(first, stretch[0, 0], none)
    early[THERMAL_GAIN] = jnp.where(first, gain, none)
    store_lines(
        edges([[state[f, k] for k in range(LEVELS_HERE)] for f in range(FIELDS)], [flow[0], flow[1]], turned), edge
    )


def step(fields, flow, mix, mix_low, mix_high, spread_y, lines, above, below):
    rows = spread_y.shape[0]
    for f in range(FIELDS):
        top, bottom = fields(f)
        face = mix[0] * (bottom - top)
        new_top = horizontal(top, flow[0], spread_y, to_column(lines[f : f + 1, :], rows, 0))
        new_top = new_top + (face - mix_high * (top - above(f)))
        new_bottom = horizontal(bottom, flow[1], spread_y, to_column(lines[f : f + 1, :], rows, rows))
        new_bottom = new_bottom + (mix_low * (below(f) - bottom) - face)
        yield f, new_top, new_bottom


def step_one_kernel(
    turned_ref, state, flow, mix, stretch, spread, weight, flipped, crossed, edge, early,
    own, to_flip, to_other, column_out,
):
    _, last, low, _ = place(turned_ref)
    mix_low = jnp.where(last, 0.0, mix[1])
    mix_high = jnp.where(low, crossed[FIELDS], flipped[FIELDS])
    column = None
    for f, top, bottom in step(
        lambda f: (state[f, 0], state[f, 1]), flow, mix, mix_low, mix_high, masked_spread(spread), edge,
        lambda f: jnp.where(low, crossed[f], flipped[f]),
        lambda f: jnp.where(low, flipped[f], crossed[f]),
    ):
        own[f, 0] = top
        own[f, 1] = bottom
        to_flip[f] = jnp.where(low, bottom, top)
        to_other[f] = jnp.where(low, top, bottom)
        term = stretch[f, 0] * top + stretch[f, 1] * bottom
        column = term if column is None else column + term
    to_flip[FIELDS] = jnp.where(low, weight[1], weight[0])
    to_other[FIELDS] = jnp.where(low, weight[0], weight[1])
    to_flip[FIELDS + 1] = mix[0]
    to_other[FIELDS + 1] = mix[0]
    for n in range(EARLY):
        to_flip[MIDDLE + n] = early[n]
    column_out[0] = column


def middle_state(first, own, thermal, height, flow, weight, mix, spread_y, last):
    fields = [[own[f, k] for k in range(LEVELS_HERE)] for f in range(FIELDS)]
    moved = horizontal(thermal, flow[0], spread_y, last) - mix[0] * thermal
    fields[0][0] = fields[0][0] + jnp.where(first, moved, 0.0)
    fields[0][1] = fields[0][1] + jnp.where(first, mix[0] * thermal, 0.0)
    for k in range(LEVELS_HERE):
        fields[2][k] = fields[2][k] + weight[k] * height
    return fields


def edge_kernel(turned_ref, own, half, other, early, flipped, elevation, flow, mix, spread, weight, edge):
    lev, _, _, turned = place(turned_ref)
    rows = spread.shape[0]
    height = elevation[...] + (half[MAP_HEIGHT] + other[MAP_HEIGHT])
    thermal = half[MAP_THERMAL] + other[MAP_THERMAL]
    flow_top = early[FLOW_TOP] + flipped[MIDDLE + FLOW_TOP]
    fields = middle_state(
        lev == 0, own, thermal, height, flow, weight, mix, masked_spread(spread), jnp.zeros((rows, 1), jnp.float32)
    )
    lines = edges(fields, [flow[0], flow[1]], turned)
    lines.append(to_line(flow_top * thermal, turned, 0))
    store_lines(lines, edge)


def step_two_kernel(
    turned_ref, own, half, other, early, column, column_other, elevation, flow, mix, spread, weight,
    flipped, crossed, old_flipped, old_crossed, edge, out_state, out_height,
):
    lev, last, low, _ = place(turned_ref)
    rows = spread.shape[0]
    spread_y = masked_spread(spread)
    mix_low = jnp.where(last, 0.0, mix[1])
    mix_high = jnp.where(low, old_crossed[FIELDS], old_flipped[FIELDS])
    weight_above = jnp.where(low, crossed[FIELDS], flipped[FIELDS])
    weight_below = jnp.where(low, flipped[FIELDS], crossed[FIELDS])

    def total(n):
        return early[n] + flipped[MIDDLE + n]

    thermal = half[MAP_THERMAL] + other[MAP_THERMAL]
    height = elevation[...] + (half[MAP_HEIGHT] + other[MAP_HEIGHT])
    stretch_top = total(STRETCH_TOP)
    seam = to_column(edge[FIELDS : FIELDS + 1, :], rows, 0)
    fields = middle_state(lev == 0, own, thermal, height, flow, weight, mix, spread_y, seam)
    height_one = height + total(STEP_ONE) + stretch_top * thermal

    def above(f):
        value = jnp.where(low, crossed[f], flipped[f])
        if f == 0:
            value = value + jnp.where(lev == 1, flipped[FIELDS + 1] * thermal, 0.0)
        return value + weight_above * height if f == 2 else value

    def below(f):
        value = jnp.where(low, flipped[f], crossed[f])
        return value + weight_below * height if f == 2 else value

    for f, top, bottom in step(
        lambda f: fields[f], flow, mix, mix_low, mix_high, spread_y, edge, above, below
    ):
        out_state[f, 0] = top + weight[0] * height_one if f == 2 else top
        out_state[f, 1] = bottom + weight[1] * height_one if f == 2 else bottom
    out_height[...] = (
        height_one
        + (column[0] + column_other[0])
        + total(WEIGHTED) * height
        + total(THERMAL_GAIN) * thermal
        + stretch_top * (along_columns(total(FLOW_TOP) * thermal, seam) + across_rows(thermal, spread_y))
    )


def call(kernel, operands, shapes, smem=(), scratch=(), grant=16 << 20):
    count, outs = len(operands), len(shapes)

    def body(*refs):
        scalars, refs = refs[: len(smem)], refs[len(smem) :]
        sources, refs = refs[:count], refs[count:]
        results, refs = refs[:outs], refs[outs:]
        held, semaphores, rest = refs[:count], refs[count], refs[count + 1 :]
        copies = [pltpu.make_async_copy(s, h, semaphores.at[n]) for n, (s, h) in enumerate(zip(sources, held))]
        for copy in copies:
            copy.start()
        for copy in copies:
            copy.wait()
        kernel(*scalars, *held, *results, *rest)

    return pl.pallas_call(
        body,
        out_shape=[jax.ShapeDtypeStruct(shape, jnp.float32) for shape in shapes],
        in_specs=[pl.BlockSpec(memory_space=pltpu.SMEM)] * len(smem) + [pl.BlockSpec(memory_space=pl.ANY)] * count,
        out_specs=[pl.BlockSpec(memory_space=pltpu.VMEM)] * outs,
        scratch_shapes=[
            *(pltpu.VMEM(o.shape, o.dtype) for o in operands),
            pltpu.SemaphoreType.DMA((count,)),
            *scratch,
        ],
        compiler_params=pltpu.CompilerParams(vmem_limit_bytes=grant),
    )(*smem, *operands)


def per_device(
    costate_ending_fields,
    costate_ending_elevation,
    upstream_transport_coefficient,
    eastward_spread_coefficient,
    interface_blending_coefficient,
    thickness_sensitivity,
    layer_velocity_factor,
    western_join_turned,
    predicted_thermal_skin,
    predicted_elevation,
    measured_quantity,
    measurement_precision,
    measurement_sort,
    sampled_location,
    active_entry_numbers,
):
    rows = costate_ending_fields.shape[3]
    cols = costate_ending_fields.shape[4]
    slots = measured_quantity.shape[3]
    groups = lax.axis_size("lev")
    tiles = lax.axis_size("tile")
    flip = [(l, l ^ 1) for l in range(groups)]
    cross = [(l, l + 1) for l in range(1, groups - 1, 2)] + [(l + 1, l) for l in range(1, groups - 1, 2)]
    pair = [(l, l ^ 2) for l in range(groups)]
    mirror = [(l, groups - 2 - (l & ~1) + (l & 1)) for l in range(groups)]
    west = [(t, (t - 1) % tiles) for t in range(tiles)]
    turned = western_join_turned

    state = costate_ending_fields[:, :, 0]
    elevation = costate_ending_elevation[0]
    flow = upstream_transport_coefficient[:, 0]
    spread = eastward_spread_coefficient[0]
    mix = interface_blending_coefficient[:, 0]
    stretch = thickness_sensitivity[:, :, 0]
    weight = layer_velocity_factor[:, 0]

    field = (rows, cols)
    (packet,) = call(
        packet_kernel,
        (measured_quantity[0, 0], measurement_precision[0, 0], measurement_sort[0, 0], sampled_location[0, 0]),
        [(tiles, 4, slots)], smem=(active_entry_numbers[0, 0],), grant=60 * 1024 * 1024,
    )
    arrived = lax.all_to_all(packet, "tile", split_axis=0, concat_axis=0, tiled=True)

    to_flip, to_other, early, edge = call(
        start_kernel, (state, flow, mix, stretch, weight),
        [(HALO, *field), (HALO, *field), (EARLY, *field), (8, cols)], smem=(turned,),
    )
    early = early + lax.ppermute(early, "lev", pair)
    old_flipped = lax.ppermute(to_flip, "lev", flip)
    old_crossed = lax.ppermute(to_other, "lev", cross)
    edge = lax.ppermute(edge, "tile", west)
    early = early + lax.ppermute(early, "lev", mirror)
    (sums,) = call(
        maps_kernel, (arrived, predicted_thermal_skin[0], predicted_elevation[0]),
        [(2, *field)], scratch=[pltpu.VMEM((4 * PIECES * rows, cols), jnp.float32)],
    )
    sums = sums + lax.ppermute(sums, "lev", pair)
    own, to_flip, to_other, column = call(
        step_one_kernel,
        (state, flow, mix, stretch, spread, weight, old_flipped, old_crossed, edge, early),
        [state.shape, (MIDDLE + EARLY, *field), (MIDDLE, *field), (1, *field)], smem=(turned,),
    )
    both = jnp.concatenate([sums, column])
    both = both + lax.ppermute(both, "lev", mirror)
    flipped = lax.ppermute(to_flip, "lev", flip)
    other = lax.ppermute(both, "lev", flip)
    crossed = lax.ppermute(to_other, "lev", cross)
    column = both[STEP_TWO:] + other[STEP_TWO:]
    column_other = lax.ppermute(column, "lev", pair)
    (edge,) = call(
        edge_kernel, (own, both, other, early, flipped, elevation, flow, mix, spread, weight),
        [(8, cols)], smem=(turned,),
    )
    edge = lax.ppermute(edge, "tile", west)
    out_state, out_height = call(
        step_two_kernel,
        (own, both, other, early, column, column_other, elevation, flow, mix, spread, weight,
         flipped, crossed, old_flipped, old_crossed, edge),
        [state.shape, field], smem=(turned,),
    )
    return (out_state[:, :, None], out_height[None])


def solution(mesh):
    placed = (
        P(None, "lev", "tile", None, None),
        P("tile", None, None),
        P("lev", "tile", None, None),
        P("tile", None, None),
        P("lev", "tile", None, None),
        P(None, "lev", "tile", None, None),
        P("lev", "tile", None, None),
        P(),
        P("tile", None, None),
        P("tile", None, None),
        P("lev", "tile", None, None),
        P("lev", "tile", None, None),
        P("lev", "tile", None, None),
        P("lev", "tile", None, None),
        P("lev", "tile", None),
    )
    return jax.shard_map(
        per_device,
        mesh=mesh,
        in_specs=placed,
        out_specs=(P(None, "lev", "tile", None, None), P("tile", None, None)),
        check_vma=False,
    )
```

```python
import jax
import jax.numpy as jnp
from jax import lax
from jax.experimental import pallas as pl
from jax.experimental.pallas import tpu as pltpu
from jax.sharding import PartitionSpec as P

FIELDS = 4
LEVELS_HERE = 2
PIECES = 3
ROWS_AT_ONCE = 32
MAP_HEIGHT, MAP_THERMAL, STEP_TWO = range(3)
STEP_ONE, WEIGHTED, FLOW_TOP, STRETCH_TOP, THERMAL_GAIN = range(5)
LATE, EARLY = 3, 5
MIX, HALO = FIELDS, FIELDS + 1
WEIGHT, AFTER = FIELDS, FIELDS + 1
MIDDLE = 2 * AFTER + 1


def maps_kernel(records, thermal, elevation, ending, out, total):
    rows, cols = thermal.shape
    sources, slots = records.shape[0], records.shape[2] - cols
    half = jnp.bfloat16
    row_of = lax.broadcasted_iota(jnp.int32, (rows, slots), 0).astype(jnp.float32).astype(half)
    col_of = lax.broadcasted_iota(jnp.int32, (2 * cols, slots), 0).astype(jnp.float32).astype(half)
    nothing = jnp.zeros((rows, slots), half)
    one, zero = jnp.ones((2 * cols, slots), half), jnp.zeros((2 * cols, slots), half)
    total[...] = jnp.zeros_like(total)

    def body(i, carry):
        left, right = [], []
        for j in range(ROWS_AT_ONCE):
            weight, scaled, kind, place = (
                records[i * ROWS_AT_ONCE + j, n : n + 1, :slots] for n in range(4)
            )
            row = jnp.floor(place * (1.0 / cols))
            col = place - row * cols + kind * cols
            here = jnp.broadcast_to(row.astype(half), nothing.shape) == row_of
            parts = []
            for rest in (weight, scaled):
                for _ in range(PIECES):
                    piece = rest.astype(half)
                    rest = rest - piece.astype(jnp.float32)
                    parts.append(jnp.where(here, jnp.broadcast_to(piece, nothing.shape), nothing))
            left.append(jnp.concatenate(parts, 0))
            right.append(jnp.where(jnp.broadcast_to(col.astype(half), one.shape) == col_of, one, zero))
        total[...] += lax.dot_general(
            jnp.concatenate(left, 1),
            jnp.concatenate(right, 1),
            (((1,), (1,)), ((), ())),
            preferred_element_type=jnp.float32,
        )
        return carry

    lax.fori_loop(0, sources // ROWS_AT_ONCE, body, 0)
    weights = sum(total[n * rows : (n + 1) * rows] for n in range(PIECES))
    values = sum(total[n * rows : (n + 1) * rows] for n in range(PIECES, 2 * PIECES))
    out[MAP_THERMAL] = thermal[...] * weights[:, :cols] - values[:, :cols]
    height = elevation[...] * weights[:, cols:] - values[:, cols:]
    out[MAP_HEIGHT] = jnp.where(lax.axis_index("lev") == 0, height + ending[...], height)


def level_place():
    lev = lax.axis_index("lev")
    return lev, lev == lax.axis_size("lev") - 1, lev % 2 == 0


def place(turned_ref):
    return *level_place(), turned_ref[lax.axis_index("tile")] == 1


def along_columns(value, last):
    cols = value.shape[1]
    lane = lax.broadcasted_iota(jnp.int32, value.shape, 1)
    return jnp.where(lane == cols - 1, jnp.broadcast_to(last, value.shape), pltpu.roll(value, cols - 1, 1))


def across_rows(value, spread):
    rows = value.shape[0]
    face = spread * (pltpu.roll(value, rows - 1, 0) - value)
    return face - pltpu.roll(face, 1, 0)


def masked_spread(spread):
    row = lax.broadcasted_iota(jnp.int32, spread.shape, 0)
    return jnp.where(row < spread.shape[0] - 1, spread[...], 0.0)


def horizontal(value, flow, spread, last):
    scaled = flow * value
    return value + (along_columns(scaled, last) - scaled) + across_rows(value, spread)


def to_column(line, rows, shift):
    wide = jnp.broadcast_to(line, (rows, line.shape[1]))
    row = lax.broadcasted_iota(jnp.int32, wide.shape, 0)
    lane = lax.broadcasted_iota(jnp.int32, wide.shape, 1)
    return jnp.sum(jnp.where(lane == row + shift, wide, 0.0), axis=1, keepdims=True)


def to_line(value, turned, shift):
    rows = value.shape[0]
    row = lax.broadcasted_iota(jnp.int32, value.shape, 0)
    lane = lax.broadcasted_iota(jnp.int32, value.shape, 1)
    chosen = lane == shift + jnp.where(turned, rows - 1 - row, row)
    return jnp.sum(jnp.where(chosen, jnp.broadcast_to(value[:, :1], value.shape), 0.0), axis=0, keepdims=True)


def edges(state, flow, turned):
    rows = state[0][0].shape[0]
    lines = [
        sum(to_line(flow[k] * state[f][k], turned, k * rows) for k in range(LEVELS_HERE)) for f in range(FIELDS)
    ]
    lines[2], lines[3] = jnp.where(turned, -lines[3], lines[2]), jnp.where(turned, lines[2], lines[3])
    return lines


def store_lines(lines, out):
    rest = jnp.zeros((out.shape[0] - len(lines), out.shape[1]), jnp.float32)
    out[...] = jnp.concatenate([*lines, rest], 0)


def packet_kernel(turned_ref, counts, state, flow, measured, precision, kind, location, packet):
    _, _, _, turned = place(turned_ref)
    sources, slots = measured.shape
    lane = lax.broadcasted_iota(jnp.int32, (1, slots), 1)
    lines = edges([[state[f, k] for k in range(LEVELS_HERE)] for f in range(FIELDS)], [flow[0], flow[1]], turned)
    block = jnp.concatenate(lines, 0)
    for s in range(sources):
        weight = jnp.where(lane < counts[s], precision[s : s + 1, :], 0.0)
        packet[s, 0:1, :slots] = weight
        packet[s, 1:2, :slots] = weight * measured[s : s + 1, :]
        packet[s, 2:3, :slots] = kind[s : s + 1, :].astype(jnp.float32)
        packet[s, 3:4, :slots] = location[s : s + 1, :].astype(jnp.float32)
        packet[s, :, slots:] = block


def start_kernel(state, flow, mix, stretch, weight, to_flip, to_other, early):
    lev, _, low = level_place()
    first = lev == 0
    column = None
    for f in range(FIELDS):
        top, bottom = state[f, 0], state[f, 1]
        to_flip[f] = jnp.where(low, bottom, top)
        to_other[f] = jnp.where(low, top, bottom)
        term = stretch[f, 0] * top + stretch[f, 1] * bottom
        column = term if column is None else column + term
    to_flip[MIX] = mix[1]
    to_other[MIX] = mix[1]
    none = jnp.zeros_like(column)
    gain = stretch[0, 0] * (1.0 - flow[0] - mix[0]) + stretch[0, 1] * mix[0]
    early[STEP_ONE] = column
    early[WEIGHTED] = stretch[2, 0] * weight[0] + stretch[2, 1] * weight[1]
    early[FLOW_TOP] = jnp.where(first, flow[0], none)
    early[STRETCH_TOP] = jnp.where(first, stretch[0, 0], none)
    early[THERMAL_GAIN] = jnp.where(first, gain, none)


def step(fields, flow, mix, mix_low, mix_high, spread_y, lines, above, below):
    rows = spread_y.shape[0]
    for f in range(FIELDS):
        top, bottom = fields(f)
        face = mix[0] * (bottom - top)
        new_top = horizontal(top, flow[0], spread_y, to_column(lines[f : f + 1, :], rows, 0))
        new_top = new_top + (face - mix_high * (top - above(f)))
        new_bottom = horizontal(bottom, flow[1], spread_y, to_column(lines[f : f + 1, :], rows, rows))
        new_bottom = new_bottom + (mix_low * (below(f) - bottom) - face)
        yield f, new_top, new_bottom


def step_one_kernel(state, flow, mix, stretch, weight, spread, halo, edge, own, packed, column_out):
    _, last, low = level_place()
    mix_low = jnp.where(last, 0.0, mix[1])
    mix_high = jnp.where(low, halo[HALO + MIX], halo[MIX])
    column = None
    for f, top, bottom in step(
        lambda f: (state[f, 0], state[f, 1]), flow, mix, mix_low, mix_high, masked_spread(spread), edge,
        lambda f: jnp.where(low, halo[HALO + f], halo[f]),
        lambda f: jnp.where(low, halo[f], halo[HALO + f]),
    ):
        own[f, 0] = top
        own[f, 1] = bottom
        packed[f] = jnp.where(low, bottom, top)
        packed[AFTER + f] = jnp.where(low, top, bottom)
        term = stretch[f, 0] * top + stretch[f, 1] * bottom
        column = term if column is None else column + term
    packed[WEIGHT] = jnp.where(low, weight[1], weight[0])
    packed[AFTER + WEIGHT] = jnp.where(low, weight[0], weight[1])
    packed[2 * AFTER] = mix[0]
    column_out[0] = column


def middle_state(first, own, thermal, height, flow, weight, mix, spread_y, last):
    fields = [[own[f, k] for k in range(LEVELS_HERE)] for f in range(FIELDS)]
    moved = horizontal(thermal, flow[0], spread_y, last) - mix[0] * thermal
    fields[0][0] = fields[0][0] + jnp.where(first, moved, 0.0)
    fields[0][1] = fields[0][1] + jnp.where(first, mix[0] * thermal, 0.0)
    for k in range(LEVELS_HERE):
        fields[2][k] = fields[2][k] + weight[k] * height
    return fields


def edge_kernel(turned_ref, own, half, other, flow, mix, spread, weight, edge):
    lev, _, _, turned = place(turned_ref)
    rows = spread.shape[0]
    height = half[MAP_HEIGHT] + other[MAP_HEIGHT]
    thermal = half[MAP_THERMAL] + other[MAP_THERMAL]
    flow_top = half[LATE + FLOW_TOP] + other[LATE + FLOW_TOP]
    fields = middle_state(
        lev == 0, own, thermal, height, flow, weight, mix, masked_spread(spread), jnp.zeros((rows, 1), jnp.float32)
    )
    lines = edges(fields, [flow[0], flow[1]], turned)
    lines.append(to_line(flow_top * thermal, turned, 0))
    store_lines(lines, edge)


def step_two_kernel(
    own, half, other, column, column_other, flow, mix, spread, weight,
    flipped, crossed, halo, edge, out_state, out_height,
):
    lev, last, low = level_place()
    rows = spread.shape[0]
    spread_y = masked_spread(spread)
    mix_low = jnp.where(last, 0.0, mix[1])
    mix_high = jnp.where(low, halo[HALO + MIX], halo[MIX])
    weight_above = jnp.where(low, crossed[WEIGHT], flipped[WEIGHT])
    weight_below = jnp.where(low, flipped[WEIGHT], crossed[WEIGHT])

    def total(n):
        return half[LATE + n] + other[LATE + n]

    thermal = half[MAP_THERMAL] + other[MAP_THERMAL]
    height = half[MAP_HEIGHT] + other[MAP_HEIGHT]
    stretch_top = total(STRETCH_TOP)
    seam = to_column(edge[FIELDS : FIELDS + 1, :], rows, 0)
    fields = middle_state(lev == 0, own, thermal, height, flow, weight, mix, spread_y, seam)
    height_one = height + total(STEP_ONE) + stretch_top * thermal

    def above(f):
        value = jnp.where(low, crossed[f], flipped[f])
        if f == 0:
            value = value + jnp.where(lev == 1, flipped[2 * AFTER] * thermal, 0.0)
        return value + weight_above * height if f == 2 else value

    def below(f):
        value = jnp.where(low, flipped[f], crossed[f])
        return value + weight_below * height if f == 2 else value

    for f, top, bottom in step(
        lambda f: fields[f], flow, mix, mix_low, mix_high, spread_y, edge, above, below
    ):
        out_state[f, 0] = top + weight[0] * height_one if f == 2 else top
        out_state[f, 1] = bottom + weight[1] * height_one if f == 2 else bottom
    out_height[...] = (
        height_one
        + (column[0] + column_other[0])
        + total(WEIGHTED) * height
        + total(THERMAL_GAIN) * thermal
        + stretch_top * (along_columns(total(FLOW_TOP) * thermal, seam) + across_rows(thermal, spread_y))
    )


def call(kernel, operands, shapes, smem=(), scratch=(), grant=16 << 20, at=None):
    at = at or {}
    count, outs = len(operands), len(shapes)

    def body(*refs):
        scalars, refs = refs[: len(smem)], refs[len(smem) :]
        sources, refs = refs[:count], refs[count:]
        results, refs = refs[:outs], refs[outs:]
        held, semaphores, rest = refs[:count], refs[count], refs[count + 1 :]
        sources = [at[n][1](s) if n in at else s for n, s in enumerate(sources)]
        copies = [pltpu.make_async_copy(s, h, semaphores.at[n]) for n, (s, h) in enumerate(zip(sources, held))]
        for copy in copies:
            copy.start()
        for copy in copies:
            copy.wait()
        kernel(*scalars, *held, *results, *rest)

    return pl.pallas_call(
        body,
        out_shape=[jax.ShapeDtypeStruct(shape, jnp.float32) for shape in shapes],
        in_specs=[pl.BlockSpec(memory_space=pltpu.SMEM)] * len(smem) + [pl.BlockSpec(memory_space=pl.ANY)] * count,
        out_specs=[pl.BlockSpec(memory_space=pltpu.VMEM)] * outs,
        scratch_shapes=[
            *(pltpu.VMEM(at[n][0] if n in at else o.shape, o.dtype) for n, o in enumerate(operands)),
            pltpu.SemaphoreType.DMA((count,)),
            *scratch,
        ],
        compiler_params=pltpu.CompilerParams(vmem_limit_bytes=grant),
    )(*smem, *operands)


def per_device(
    costate_ending_fields,
    costate_ending_elevation,
    upstream_transport_coefficient,
    eastward_spread_coefficient,
    interface_blending_coefficient,
    thickness_sensitivity,
    layer_velocity_factor,
    western_join_turned,
    predicted_thermal_skin,
    predicted_elevation,
    measured_quantity,
    measurement_precision,
    measurement_sort,
    sampled_location,
    active_entry_numbers,
):
    rows = costate_ending_fields.shape[3]
    cols = costate_ending_fields.shape[4]
    slots = measured_quantity.shape[3]
    groups = lax.axis_size("lev")
    tiles = lax.axis_size("tile")
    flip = [(l, l ^ 1) for l in range(groups)]
    inward = [(l, l - 2) for l in range(2, groups, 2)] + [(l, l + 2) for l in range(1, groups - 2, 2)]
    outward = [(destination, source) for source, destination in inward]
    pair = [(l, l ^ 2) for l in range(groups)]
    mirror = [(l, groups - 2 - (l & ~1) + (l & 1)) for l in range(groups)]
    west = [(t, (t - 1) % tiles) for t in range(tiles)]
    turned = western_join_turned

    state = costate_ending_fields[:, :, 0]
    elevation = costate_ending_elevation[0]
    flow = upstream_transport_coefficient[:, 0]
    spread = eastward_spread_coefficient[0]
    mix = interface_blending_coefficient[:, 0]
    stretch = thickness_sensitivity[:, :, 0]
    weight = layer_velocity_factor[:, 0]

    field = (rows, cols)
    (packet,) = call(
        packet_kernel,
        (state, flow, measured_quantity[0, 0], measurement_precision[0, 0], measurement_sort[0, 0], sampled_location[0, 0]),
        [(tiles, 4, slots + cols)], smem=(turned, active_entry_numbers[0, 0]), grant=60 * 1024 * 1024,
    )
    arrived = lax.all_to_all(packet, "tile", split_axis=0, concat_axis=0, tiled=True)

    to_flip, to_other, early = call(
        start_kernel, (state, flow, mix, stretch, weight),
        [(HALO, *field), (HALO, *field), (EARLY, *field)],
    )
    relayed = lax.ppermute(to_other, "lev", inward)
    early = early + lax.ppermute(early, "lev", pair)
    halo = lax.ppermute(jnp.concatenate([to_flip, relayed]), "lev", flip)
    (sums,) = call(
        maps_kernel, (arrived, predicted_thermal_skin[0], predicted_elevation[0], elevation),
        [(2, *field)], grant=24 << 20,
        scratch=[pltpu.VMEM((2 * PIECES * rows, 2 * cols), jnp.float32)],
    )
    sums = sums + lax.ppermute(sums, "lev", pair)
    own, packed, column = call(
        step_one_kernel,
        (state, flow, mix, stretch, weight, spread, halo, arrived),
        [state.shape, (MIDDLE, *field), (1, *field)],
        at={
            7: (
                (4, cols),
                lambda ref: ref.at[lax.rem(lax.axis_index("tile") + 1, tiles), :, pl.ds(slots, cols)],
            )
        },
    )
    half = jnp.concatenate([sums, column, early])
    half = half + lax.ppermute(half, "lev", mirror)
    flipped = lax.ppermute(packed, "lev", flip)
    other = lax.ppermute(half, "lev", flip)
    (edge,) = call(
        edge_kernel, (own, half, other, flow, mix, spread, weight),
        [(8, cols)], smem=(turned,),
    )
    edge = lax.ppermute(edge, "tile", west)
    crossed = lax.ppermute(flipped[AFTER : 2 * AFTER], "lev", outward)
    column = half[STEP_TWO:LATE] + other[STEP_TWO:LATE]
    column_other = lax.ppermute(column, "lev", pair)
    out_state, out_height = call(
        step_two_kernel,
        (own, half, other, column, column_other, flow, mix, spread, weight,
         flipped, crossed, halo, edge),
        [state.shape, field],
    )
    return (out_state[:, :, None], out_height[None])


def solution(mesh):
    placed = (
        P(None, "lev", "tile", None, None),
        P("tile", None, None),
        P("lev", "tile", None, None),
        P("tile", None, None),
        P("lev", "tile", None, None),
        P(None, "lev", "tile", None, None),
        P("lev", "tile", None, None),
        P(),
        P("tile", None, None),
        P("tile", None, None),
        P("lev", "tile", None, None),
        P("lev", "tile", None, None),
        P("lev", "tile", None, None),
        P("lev", "tile", None, None),
        P("lev", "tile", None),
    )
    return jax.shard_map(
        per_device,
        mesh=mesh,
        in_specs=placed,
        out_specs=(P(None, "lev", "tile", None, None), P("tile", None, None)),
        check_vma=False,
    )
```

```python
import jax
import jax.numpy as jnp
from jax import lax
from jax.experimental import pallas as pl
from jax.experimental.pallas import tpu as pltpu
from jax.sharding import PartitionSpec as P

FIELDS = 4
LEVELS_HERE = 2
PIECES = 3
ROWS_AT_ONCE = 32
MAP_HEIGHT, MAP_THERMAL, STEP_TWO = range(3)
FLOW_TOP, STEP_ONE, WEIGHTED, STRETCH_TOP, THERMAL_GAIN = range(5)
LATE, EARLY = 3, 5
SOON = LATE + 1
MIX, HALO = FIELDS, FIELDS + 1
WEIGHT, UPPER, AFTER = FIELDS, FIELDS + 1, FIELDS + 2


def maps_kernel(records, thermal, elevation, ending, out, total):
    rows, cols = thermal.shape
    sources, slots = records.shape[0], records.shape[2] - cols
    half = jnp.bfloat16
    row_of = lax.broadcasted_iota(jnp.int32, (rows, slots), 0).astype(jnp.float32).astype(half)
    col_of = lax.broadcasted_iota(jnp.int32, (2 * cols, slots), 0).astype(jnp.float32).astype(half)
    nothing = jnp.zeros((rows, slots), half)
    one, zero = jnp.ones((2 * cols, slots), half), jnp.zeros((2 * cols, slots), half)
    total[...] = jnp.zeros_like(total)

    def body(i, carry):
        left, right = [], []
        for j in range(ROWS_AT_ONCE):
            weight, scaled, kind, place = (
                records[i * ROWS_AT_ONCE + j, n : n + 1, :slots] for n in range(4)
            )
            row = jnp.floor(place * (1.0 / cols))
            col = place - row * cols + kind * cols
            here = jnp.broadcast_to(row.astype(half), nothing.shape) == row_of
            parts = []
            for rest in (weight, scaled):
                for _ in range(PIECES):
                    piece = rest.astype(half)
                    rest = rest - piece.astype(jnp.float32)
                    parts.append(jnp.where(here, jnp.broadcast_to(piece, nothing.shape), nothing))
            left.append(jnp.concatenate(parts, 0))
            right.append(jnp.where(jnp.broadcast_to(col.astype(half), one.shape) == col_of, one, zero))
        total[...] += lax.dot_general(
            jnp.concatenate(left, 1),
            jnp.concatenate(right, 1),
            (((1,), (1,)), ((), ())),
            preferred_element_type=jnp.float32,
        )
        return carry

    lax.fori_loop(0, sources // ROWS_AT_ONCE, body, 0)
    weights = sum(total[n * rows : (n + 1) * rows] for n in range(PIECES))
    values = sum(total[n * rows : (n + 1) * rows] for n in range(PIECES, 2 * PIECES))
    out[MAP_THERMAL] = thermal[...] * weights[:, :cols] - values[:, :cols]
    height = elevation[...] * weights[:, cols:] - values[:, cols:]
    out[MAP_HEIGHT] = jnp.where(lax.axis_index("lev") == 0, height + ending[...], height)


def level_place():
    lev = lax.axis_index("lev")
    return lev, lev == lax.axis_size("lev") - 1, lev % 2 == 0


def place(turned_ref):
    return *level_place(), turned_ref[lax.axis_index("tile")] == 1


def along_columns(value, last):
    cols = value.shape[1]
    lane = lax.broadcasted_iota(jnp.int32, value.shape, 1)
    return jnp.where(lane == cols - 1, jnp.broadcast_to(last, value.shape), pltpu.roll(value, cols - 1, 1))


def across_rows(value, spread):
    rows = value.shape[0]
    face = spread * (pltpu.roll(value, rows - 1, 0) - value)
    return face - pltpu.roll(face, 1, 0)


def masked_spread(spread):
    row = lax.broadcasted_iota(jnp.int32, spread.shape, 0)
    return jnp.where(row < spread.shape[0] - 1, spread[...], 0.0)


def horizontal(value, flow, spread, last):
    scaled = flow * value
    return value + (along_columns(scaled, last) - scaled) + across_rows(value, spread)


def to_column(line, rows, shift):
    wide = jnp.broadcast_to(line, (rows, line.shape[1]))
    row = lax.broadcasted_iota(jnp.int32, wide.shape, 0)
    lane = lax.broadcasted_iota(jnp.int32, wide.shape, 1)
    return jnp.sum(jnp.where(lane == row + shift, wide, 0.0), axis=1, keepdims=True)


def to_line(value, turned, shift):
    rows = value.shape[0]
    row = lax.broadcasted_iota(jnp.int32, value.shape, 0)
    lane = lax.broadcasted_iota(jnp.int32, value.shape, 1)
    chosen = lane == shift + jnp.where(turned, rows - 1 - row, row)
    return jnp.sum(jnp.where(chosen, jnp.broadcast_to(value[:, :1], value.shape), 0.0), axis=0, keepdims=True)


def edges(state, flow, turned):
    rows = state[0][0].shape[0]
    lines = [
        sum(to_line(flow[k] * state[f][k], turned, k * rows) for k in range(LEVELS_HERE)) for f in range(FIELDS)
    ]
    lines[2], lines[3] = jnp.where(turned, -lines[3], lines[2]), jnp.where(turned, lines[2], lines[3])
    return lines


def store_lines(lines, out):
    rest = jnp.zeros((out.shape[0] - len(lines), out.shape[1]), jnp.float32)
    out[...] = jnp.concatenate([*lines, rest], 0)


def packet_kernel(turned_ref, counts, state, flow, measured, precision, kind, location, packet):
    _, _, _, turned = place(turned_ref)
    sources, slots = measured.shape
    lane = lax.broadcasted_iota(jnp.int32, (1, slots), 1)
    lines = edges([[state[f, k] for k in range(LEVELS_HERE)] for f in range(FIELDS)], [flow[0], flow[1]], turned)
    block = jnp.concatenate(lines, 0)
    for s in range(sources):
        weight = jnp.where(lane < counts[s], precision[s : s + 1, :], 0.0)
        packet[s, 0:1, :slots] = weight
        packet[s, 1:2, :slots] = weight * measured[s : s + 1, :]
        packet[s, 2:3, :slots] = kind[s : s + 1, :].astype(jnp.float32)
        packet[s, 3:4, :slots] = location[s : s + 1, :].astype(jnp.float32)
        packet[s, :, slots:] = block


def start_kernel(state, flow, mix, stretch, weight, to_flip, to_other, early):
    lev, _, low = level_place()
    first = lev == 0
    column = None
    for f in range(FIELDS):
        top, bottom = state[f, 0], state[f, 1]
        to_flip[f] = jnp.where(low, bottom, top)
        to_other[f] = jnp.where(low, top, bottom)
        term = stretch[f, 0] * top + stretch[f, 1] * bottom
        column = term if column is None else column + term
    to_flip[MIX] = mix[1]
    to_other[MIX] = mix[1]
    none = jnp.zeros_like(column)
    gain = stretch[0, 0] * (1.0 - flow[0] - mix[0]) + stretch[0, 1] * mix[0]
    early[STEP_ONE] = column
    early[WEIGHTED] = stretch[2, 0] * weight[0] + stretch[2, 1] * weight[1]
    early[FLOW_TOP] = jnp.where(first, flow[0], none)
    early[STRETCH_TOP] = jnp.where(first, stretch[0, 0], none)
    early[THERMAL_GAIN] = jnp.where(first, gain, none)


def step(fields, flow, mix, mix_low, mix_high, spread_y, lines, above, below):
    rows = spread_y.shape[0]
    for f in range(FIELDS):
        top, bottom = fields(f)
        face = mix[0] * (bottom - top)
        new_top = horizontal(top, flow[0], spread_y, to_column(lines[f : f + 1, :], rows, 0))
        new_top = new_top + (face - mix_high * (top - above(f)))
        new_bottom = horizontal(bottom, flow[1], spread_y, to_column(lines[f : f + 1, :], rows, rows))
        new_bottom = new_bottom + (mix_low * (below(f) - bottom) - face)
        yield f, new_top, new_bottom


def step_one_kernel(state, flow, mix, stretch, weight, spread, halo, edge, own, to_flip, to_other, column_out):
    _, last, low = level_place()
    mix_low = jnp.where(last, 0.0, mix[1])
    mix_high = jnp.where(low, halo[HALO + MIX], halo[MIX])
    column = None
    for f, top, bottom in step(
        lambda f: (state[f, 0], state[f, 1]), flow, mix, mix_low, mix_high, masked_spread(spread), edge,
        lambda f: jnp.where(low, halo[HALO + f], halo[f]),
        lambda f: jnp.where(low, halo[f], halo[HALO + f]),
    ):
        own[f, 0] = top
        own[f, 1] = bottom
        to_flip[f] = jnp.where(low, bottom, top)
        to_other[f] = jnp.where(low, top, bottom)
        term = stretch[f, 0] * top + stretch[f, 1] * bottom
        column = term if column is None else column + term
    to_flip[WEIGHT] = jnp.where(low, weight[1], weight[0])
    to_other[WEIGHT] = jnp.where(low, weight[0], weight[1])
    to_flip[UPPER] = mix[0]
    column_out[0] = column


def middle_state(first, own, thermal, height, flow, weight, mix, spread_y, last):
    fields = [[own[f, k] for k in range(LEVELS_HERE)] for f in range(FIELDS)]
    moved = horizontal(thermal, flow[0], spread_y, last) - mix[0] * thermal
    fields[0][0] = fields[0][0] + jnp.where(first, moved, 0.0)
    fields[0][1] = fields[0][1] + jnp.where(first, mix[0] * thermal, 0.0)
    for k in range(LEVELS_HERE):
        fields[2][k] = fields[2][k] + weight[k] * height
    return fields


def edge_kernel(turned_ref, own, half, other, flow, mix, spread, weight, edge):
    lev, _, _, turned = place(turned_ref)
    rows = spread.shape[0]
    height = half[MAP_HEIGHT] + other[MAP_HEIGHT]
    thermal = half[MAP_THERMAL] + other[MAP_THERMAL]
    flow_top = half[LATE + FLOW_TOP] + other[LATE + FLOW_TOP]
    fields = middle_state(
        lev == 0, own, thermal, height, flow, weight, mix, masked_spread(spread), jnp.zeros((rows, 1), jnp.float32)
    )
    lines = edges(fields, [flow[0], flow[1]], turned)
    lines.append(to_line(flow_top * thermal, turned, 0))
    store_lines(lines, edge)


def step_two_kernel(
    own, half, other, column, column_other, flow, mix, spread, weight,
    middle, halo, edge, out_state, out_height,
):
    lev, last, low = level_place()
    rows = spread.shape[0]
    spread_y = masked_spread(spread)
    mix_low = jnp.where(last, 0.0, mix[1])
    mix_high = jnp.where(low, halo[HALO + MIX], halo[MIX])
    weight_above = jnp.where(low, middle[AFTER + WEIGHT], middle[WEIGHT])
    weight_below = jnp.where(low, middle[WEIGHT], middle[AFTER + WEIGHT])

    def total(n):
        return half[LATE + n] + (other[LATE] if n == FLOW_TOP else middle[2 * AFTER - 2 + n])

    thermal = half[MAP_THERMAL] + other[MAP_THERMAL]
    height = half[MAP_HEIGHT] + other[MAP_HEIGHT]
    stretch_top = total(STRETCH_TOP)
    seam = to_column(edge[FIELDS : FIELDS + 1, :], rows, 0)
    fields = middle_state(lev == 0, own, thermal, height, flow, weight, mix, spread_y, seam)
    height_one = height + total(STEP_ONE) + stretch_top * thermal

    def above(f):
        value = jnp.where(low, middle[AFTER + f], middle[f])
        if f == 0:
            value = value + jnp.where(lev == 1, middle[UPPER] * thermal, 0.0)
        return value + weight_above * height if f == 2 else value

    def below(f):
        value = jnp.where(low, middle[f], middle[AFTER + f])
        return value + weight_below * height if f == 2 else value

    for f, top, bottom in step(
        lambda f: fields[f], flow, mix, mix_low, mix_high, spread_y, edge, above, below
    ):
        out_state[f, 0] = top + weight[0] * height_one if f == 2 else top
        out_state[f, 1] = bottom + weight[1] * height_one if f == 2 else bottom
    out_height[...] = (
        height_one
        + (column[0] + column_other[0])
        + total(WEIGHTED) * height
        + total(THERMAL_GAIN) * thermal
        + stretch_top * (along_columns(total(FLOW_TOP) * thermal, seam) + across_rows(thermal, spread_y))
    )


def call(kernel, operands, shapes, smem=(), scratch=(), grant=16 << 20, at=None):
    at = at or {}
    count, outs = len(operands), len(shapes)

    def body(*refs):
        scalars, refs = refs[: len(smem)], refs[len(smem) :]
        sources, refs = refs[:count], refs[count:]
        results, refs = refs[:outs], refs[outs:]
        held, semaphores, rest = refs[:count], refs[count], refs[count + 1 :]
        sources = [at[n][1](s) if n in at else s for n, s in enumerate(sources)]
        copies = [pltpu.make_async_copy(s, h, semaphores.at[n]) for n, (s, h) in enumerate(zip(sources, held))]
        for copy in copies:
            copy.start()
        for copy in copies:
            copy.wait()
        kernel(*scalars, *held, *results, *rest)

    return pl.pallas_call(
        body,
        out_shape=[jax.ShapeDtypeStruct(shape, jnp.float32) for shape in shapes],
        in_specs=[pl.BlockSpec(memory_space=pltpu.SMEM)] * len(smem) + [pl.BlockSpec(memory_space=pl.ANY)] * count,
        out_specs=[pl.BlockSpec(memory_space=pltpu.VMEM)] * outs,
        scratch_shapes=[
            *(pltpu.VMEM(at[n][0] if n in at else o.shape, o.dtype) for n, o in enumerate(operands)),
            pltpu.SemaphoreType.DMA((count,)),
            *scratch,
        ],
        compiler_params=pltpu.CompilerParams(vmem_limit_bytes=grant),
    )(*smem, *operands)


def per_device(
    costate_ending_fields,
    costate_ending_elevation,
    upstream_transport_coefficient,
    eastward_spread_coefficient,
    interface_blending_coefficient,
    thickness_sensitivity,
    layer_velocity_factor,
    western_join_turned,
    predicted_thermal_skin,
    predicted_elevation,
    measured_quantity,
    measurement_precision,
    measurement_sort,
    sampled_location,
    active_entry_numbers,
):
    rows = costate_ending_fields.shape[3]
    cols = costate_ending_fields.shape[4]
    slots = measured_quantity.shape[3]
    groups = lax.axis_size("lev")
    tiles = lax.axis_size("tile")
    flip = [(l, l ^ 1) for l in range(groups)]
    inward = [(l, l - 2) for l in range(2, groups, 2)] + [(l, l + 2) for l in range(1, groups - 2, 2)]
    pair = [(l, l ^ 2) for l in range(groups)]
    mirror = [(l, groups - 2 - (l & ~1) + (l & 1)) for l in range(groups)]
    west = [(t, (t - 1) % tiles) for t in range(tiles)]
    turned = western_join_turned

    state = costate_ending_fields[:, :, 0]
    elevation = costate_ending_elevation[0]
    flow = upstream_transport_coefficient[:, 0]
    spread = eastward_spread_coefficient[0]
    mix = interface_blending_coefficient[:, 0]
    stretch = thickness_sensitivity[:, :, 0]
    weight = layer_velocity_factor[:, 0]

    field = (rows, cols)
    (packet,) = call(
        packet_kernel,
        (state, flow, measured_quantity[0, 0], measurement_precision[0, 0], measurement_sort[0, 0], sampled_location[0, 0]),
        [(tiles, 4, slots + cols)], smem=(turned, active_entry_numbers[0, 0]), grant=60 * 1024 * 1024,
    )
    arrived = lax.all_to_all(packet, "tile", split_axis=0, concat_axis=0, tiled=True)

    to_flip, to_other, early = call(
        start_kernel, (state, flow, mix, stretch, weight),
        [(HALO, *field), (HALO, *field), (EARLY, *field)],
    )
    relayed = lax.ppermute(to_other, "lev", inward)
    early = early + lax.ppermute(early, "lev", pair)
    halo = lax.ppermute(jnp.concatenate([to_flip, relayed]), "lev", flip)
    (sums,) = call(
        maps_kernel, (arrived, predicted_thermal_skin[0], predicted_elevation[0], elevation),
        [(2, *field)], grant=24 << 20,
        scratch=[pltpu.VMEM((2 * PIECES * rows, 2 * cols), jnp.float32)],
    )
    sums = sums + lax.ppermute(sums, "lev", pair)
    own, to_flip, to_other, column = call(
        step_one_kernel,
        (state, flow, mix, stretch, weight, spread, halo, arrived),
        [state.shape, (AFTER, *field), (AFTER - 1, *field), (1, *field)],
        at={
            7: (
                (4, cols),
                lambda ref: ref.at[lax.rem(lax.axis_index("tile") + 1, tiles), :, pl.ds(slots, cols)],
            )
        },
    )
    half = jnp.concatenate([sums, column, early])
    half = half + lax.ppermute(half, "lev", mirror)
    relayed = lax.ppermute(to_other, "lev", inward)
    other = lax.ppermute(half[:SOON], "lev", flip)
    middle = lax.ppermute(jnp.concatenate([to_flip, relayed, half[SOON:]]), "lev", flip)
    (edge,) = call(
        edge_kernel, (own, half, other, flow, mix, spread, weight),
        [(8, cols)], smem=(turned,),
    )
    edge = lax.ppermute(edge, "tile", west)
    column = half[STEP_TWO:LATE] + other[STEP_TWO:LATE]
    column_other = lax.ppermute(column, "lev", pair)
    out_state, out_height = call(
        step_two_kernel,
        (own, half, other, column, column_other, flow, mix, spread, weight,
         middle, halo, edge),
        [state.shape, field],
    )
    return (out_state[:, :, None], out_height[None])


def solution(mesh):
    placed = (
        P(None, "lev", "tile", None, None),
        P("tile", None, None),
        P("lev", "tile", None, None),
        P("tile", None, None),
        P("lev", "tile", None, None),
        P(None, "lev", "tile", None, None),
        P("lev", "tile", None, None),
        P(),
        P("tile", None, None),
        P("tile", None, None),
        P("lev", "tile", None, None),
        P("lev", "tile", None, None),
        P("lev", "tile", None, None),
        P("lev", "tile", None, None),
        P("lev", "tile", None),
    )
    return jax.shard_map(
        per_device,
        mesh=mesh,
        in_specs=placed,
        out_specs=(P(None, "lev", "tile", None, None), P("tile", None, None)),
        check_vma=False,
    )
```
